32 devices in a mesh: slab: 4 (over y, x), mem: 8 (over z, core).
Axes of the slice: x: 2, y: 2, z: 4, core: 2. Of those that a mesh axis runs over, the one named last changes fastest.
Arguments:
- ensemble: bfloat16 [1024, 32, 1024], P('mem', 'slab'), may hold values from -6 to 6
- diffusivity: float32 [32, 1024], P('slab'), may hold values from 0.05 to 0.2
- zonal_velocity: float32 [32, 1024], P('slab'), may hold values from -0.5 to 0.5
- obs_anomalies: bfloat16 [1024, 64, 128], P('mem', 'slab'), may hold values from -6 to 6
- innovations: bfloat16 [1024, 64, 128], P('mem', 'slab'), may hold values from -6 to 6
- block_lists: int32 [32, 4], P('slab'), may hold values from 0 to 15
- block_counts: int32 [32], P('slab'), may hold values from 1 to 4, 80 in all
- patch_links: int32 [32, 2], P(('slab', 'mem')), may hold values 0 or 1
Outputs:
- analysis: bfloat16 [1024, 32, 1024], P('mem', 'slab')
The draws below stay inside these ranges and needn't reach their ends.
Inputs may be any that keep to these rules, and one draw needn't show every extreme that they name: `block_lists`: entries past a patch's count are not used. `block_counts`: some patch uses all 4 entries.
All inputs are finite; a program needn't handle non-finite values. No bound on the sum of `block_counts` or of `patch_links` on one device may be relied on, other than what follows from the above.
Results may differ from the reference program's by a relative error of at most 0.0046.
The reference program's roundings to bfloat16 on the way count: a program that leaves them out, or rounds other values in their place, can miss the bound.
Values may be sent and summed in bfloat16 or wider, within the bound.
A program may use at most 128 MiB of HBM per device.

```python
import math
import jax
import jax.numpy as jnp
import numpy as np
from jax import lax

M = 1024
PATCH_PTS = 1024
BLOCK = 128
LIST = 4
ROWS_SLAB = 8
ROWS = 32
OBS_SLAB = 16
OBS_BLOCKS = 64


def place_ends(entries, rng, low, high):
    dims = entries.shape
    spot = [jax.random.randint(jax.random.fold_in(rng, axis), (), 0, dims[axis]) for axis in range(len(dims))]
    entries = entries.at[tuple(spot)].set(low)
    longest = dims.index(max(dims))
    spot[longest] = (spot[longest] + 1) % dims[longest]
    return entries.at[tuple(spot)].set(high)


def block_scale(stream_key, dims, cuts, smallest, high):
    gain, own = 1.0, jax.random.fold_in(stream_key, 6)
    for dim, blocks in cuts:
        heights = jnp.exp(jax.random.uniform(jax.random.fold_in(own, dim), (blocks,), jnp.float32, smallest / len(cuts), high / len(cuts)))
        gain = gain * jnp.repeat(heights, dims[dim] // blocks).reshape([-1 if axis == dim else 1 for axis in range(len(dims))])
    return gain


def length_profile(count, total, reach, lean):
    weights = [(1 << 20) // math.isqrt(standing ** lean) + 1 for standing in range(2, count + 1)]
    surplus, counts = total - reach - (count - 1), [1] * (count - 1)
    while surplus > 0:
        movable = [i for i in range(count - 1) if counts[i] < reach]
        whole, remaining = sum([weights[i] for i in movable]), surplus
        for i in movable:
            more = min(reach - counts[i], max(1, remaining * weights[i] // whole), surplus)
            counts[i] = counts[i] + more
            surplus = surplus - more
    return np.array([reach] + counts)


def uneven_parts(stream_key, number_of, total, reach, slope):
    if number_of == 2:
        one = jax.random.randint(stream_key, (), max(1, total - reach), min(reach, total - 1) + 1)
        return jnp.stack([one, total - one])
    lengths = jnp.asarray(length_profile(number_of, total, reach, slope), jnp.int32)
    pairs = (number_of - 1) // 2
    source_of, sink = lengths[1:1 + 2 * pairs:2], lengths[2:2 + 2 * pairs:2]
    margin = jnp.minimum(source_of - 1, reach - sink)
    moved = jax.random.randint(jax.random.fold_in(stream_key, 1), (pairs,), 0, 1 << 20) % (margin + 1)
    lengths = lengths.at[1:1 + 2 * pairs:2].set(source_of - moved).at[2:2 + 2 * pairs:2].set(sink + moved)
    return lengths[jax.random.permutation(jax.random.fold_in(stream_key, 2), number_of)]


def scatter_about(rng, shape, width, limit, shards=(), kind=jnp.bfloat16):
    factor_of = block_scale(rng, shape, shards, -0.22, 0.18) if shards else 1.0
    array = jax.random.normal(rng, shape, jnp.float32) * width * factor_of
    return jnp.minimum(jnp.maximum(array, -limit), limit).astype(kind)


def setup_inputs(seed: int = 0) -> dict:
    key_of = jax.random.split(jax.random.key(seed), 9)
    return {
        "ensemble": scatter_about(key_of[0], (M, ROWS, PATCH_PTS), 1.0, 6.0, ((0, 8), (1, 4))),
        "diffusivity": jnp.clip(jnp.exp(math.log(0.2) - 1.3862944 * jax.random.uniform(key_of[1], (ROWS, PATCH_PTS), jnp.float32) ** block_scale(key_of[1], (ROWS, PATCH_PTS), ((0, 4),), -0.2, 0.2)), 0.05, 0.2),
        "zonal_velocity": jnp.clip(jax.random.uniform(key_of[2], (ROWS, PATCH_PTS), jnp.float32, -0.5, 0.5) * block_scale(key_of[2], (ROWS, PATCH_PTS), ((0, 4),), -0.4, 0.0), -0.5, 0.5),
        "obs_anomalies": scatter_about(key_of[3], (M, OBS_BLOCKS, BLOCK), 1.0, 6.0, ((0, 8), (1, 4))),
        "innovations": scatter_about(key_of[4], (M, OBS_BLOCKS, BLOCK), 1.0, 6.0, ((0, 8), (1, 4))),
        "block_lists": place_ends(jax.random.randint(key_of[5], (ROWS, LIST), 0, OBS_SLAB), jax.random.fold_in(key_of[5], 1), 0, OBS_SLAB - 1).astype(jnp.int32),
        "block_counts": uneven_parts(key_of[6], ROWS, 5 * ROWS // 2, LIST, 0).astype(jnp.int32),
        "patch_links": place_ends((jax.random.randint(key_of[7], (ROWS, 2), 0, 4) < 3).astype(jnp.int32), jax.random.fold_in(key_of[7], 1), 0, 1),
    }


def reference(ensemble, diffusivity, zonal_velocity, obs_anomalies, innovations, block_lists, block_counts, patch_links):

    def member_advance(member):
        values = member.astype(jnp.float32)
        padded = jnp.pad(values, ((1, 1), (0, 0)))
        north_rows = padded[:-2, :]
        south_rows = padded[2:, :]
        east_cells = jnp.roll(values, -1, axis=1)
        west_cells = jnp.roll(values, 1, axis=1)
        tendency = diffusivity * (north_rows + south_rows + east_cells + west_cells - 4.0 * values) - zonal_velocity * (east_cells - west_cells) * 0.5
        return (values + tendency).astype(jnp.bfloat16)
    prior_state = lax.map(member_advance, ensemble)

    def patch_gain(patch_number):
        slab_first = patch_number // ROWS_SLAB * OBS_SLAB
        chosen = (slab_first + block_lists[patch_number]).astype(jnp.int32)
        present = (jnp.arange(LIST) < block_counts[patch_number]).astype(jnp.float32)[None, :, None]
        anomaly = (jnp.take(obs_anomalies, chosen, axis=1).astype(jnp.float32) * present).reshape(M, LIST * BLOCK)
        innovation = (jnp.take(innovations, chosen, axis=1).astype(jnp.float32) * present).reshape(M, LIST * BLOCK)
        gram_matrix = jnp.dot(anomaly, anomaly.T, precision=lax.Precision.HIGHEST) + (M - 1.0) * jnp.eye(M, dtype=jnp.float32)
        cross_term = jnp.dot(anomaly, innovation.T, precision=lax.Precision.HIGHEST)
        factor = jnp.linalg.cholesky(gram_matrix)
        halfway = lax.linalg.triangular_solve(factor, cross_term, left_side=True, lower=True)
        gain_matrix = lax.linalg.triangular_solve(factor, halfway, left_side=True, lower=True, transpose_a=True)
        return gain_matrix.astype(jnp.bfloat16)
    gains = lax.map(patch_gain, jnp.arange(ROWS))
    bordered = jnp.pad(gains, ((1, 1), (0, 0), (0, 0)))

    def patch_update(patch_number):
        upper_flag = 0.5 + 0.5 * patch_links[patch_number, 0].astype(jnp.float32)
        lower_flag = 0.5 + 0.5 * patch_links[patch_number, 1].astype(jnp.float32)
        before = lax.dynamic_index_in_dim(bordered, patch_number, 0, keepdims=False).astype(jnp.float32)
        middle = lax.dynamic_index_in_dim(bordered, patch_number + 1, 0, keepdims=False).astype(jnp.float32)
        after = lax.dynamic_index_in_dim(bordered, patch_number + 2, 0, keepdims=False).astype(jnp.float32)
        smoothed = ((middle + upper_flag * before + lower_flag * after) / (1.0 + upper_flag + lower_flag)).astype(jnp.bfloat16)
        column_grid = lax.dynamic_index_in_dim(prior_state, patch_number, 1, keepdims=False).astype(jnp.float32)
        update = jnp.dot(smoothed.astype(jnp.float32).T, column_grid, precision=lax.Precision.HIGHEST)
        return (column_grid + update).astype(jnp.bfloat16)
    analysed = lax.map(patch_update, jnp.arange(ROWS))
    return jnp.transpose(analysed, (1, 0, 2))
```

```python
import functools

import jax
import jax.numpy as jnp
from jax import lax
from jax.experimental import pallas as pl
from jax.experimental.pallas import tpu as pltpu
from jax.sharding import PartitionSpec as P

F32, BF16 = jnp.float32, jnp.bfloat16
VMEM_SPEC = pl.BlockSpec(memory_space=pltpu.VMEM)
SMEM_SPEC = pl.BlockSpec(memory_space=pltpu.SMEM)
ANY_SPEC = pl.BlockSpec(memory_space=pl.ANY)
MESH = pl.DeviceIdType.MESH


def mm(a, b, dims, precision=None):
    return lax.dot_general(a, b, (dims, ((), ())), precision=precision, preferred_element_type=F32)


def pick_kernel(blocks, lists, counts, anom, innov, out, wide):
    patches, width = lists.shape
    members = out.shape[2]
    block = anom.shape[1]
    wide[0] = anom[...].astype(F32)
    wide[1] = innov[...].astype(F32)

    def patch(p, carry):
        for j in range(width):
            entry = lists[p, j]
            keep = (j < counts[p]).astype(F32)
            for kind in range(2):
                rows = wide[kind, pl.ds(entry, members, stride=blocks), :]
                out[p, kind, :, j * block:(j + 1) * block] = (rows * keep).astype(BF16)
        return carry

    lax.fori_loop(0, patches, patch, 0)


def pick(anom, innov, lists, counts):
    members, blocks, block = anom.shape
    patches, width = lists.shape
    return pl.pallas_call(
        functools.partial(pick_kernel, blocks),
        out_shape=jax.ShapeDtypeStruct((patches, 2, members, width * block), BF16),
        in_specs=[SMEM_SPEC, SMEM_SPEC, VMEM_SPEC, VMEM_SPEC],
        out_specs=VMEM_SPEC,
        scratch_shapes=[pltpu.VMEM((2, members * blocks, block), F32)],
    )(lists, counts, anom.reshape(-1, block), innov.reshape(-1, block))


def gain_kernel(yz, gain, a_ref, x_ref, w_ref):
    n, _, part, size = yz.shape
    members = n * part
    shift = members - 1.0
    anom = yz[:, 0].reshape(members, size)
    diag = lax.broadcasted_iota(jnp.int32, (size, size), 0) == lax.broadcasted_iota(jnp.int32, (size, size), 1)
    eye = jnp.where(diag, 1.0, 0.0).astype(F32)
    a = mm(anom, anom, ((0,), (0,))) + shift * eye
    a_ref[...] = a
    bound = jnp.max(jnp.sum(jnp.abs(a), axis=0, keepdims=True))
    start = 2.0 / (shift + bound)
    x_ref[...] = (2.0 * start) * eye - (start * start) * a

    def rough(i, carry):
        x = x_ref[...]
        xb = x.astype(BF16)
        r = eye - mm(a_ref[...].astype(BF16), xb, ((1,), (0,)))
        x_ref[...] = x + mm(xb, r.astype(BF16), ((1,), (0,)))
        return carry

    lax.fori_loop(0, 5, rough, 0)

    def norm(r):
        return jnp.max(jnp.sum(jnp.abs(r), axis=0, keepdims=True))

    def residual():
        return eye - mm(a_ref[...], x_ref[...], ((1,), (0,)), lax.Precision.HIGHEST)

    w_ref[...] = residual()
    first = norm(w_ref[...])

    @pl.when(jnp.logical_not(first < 0.5))
    def _():
        x_ref[...] = start * eye
        w_ref[...] = residual()

    def more(state):
        i, r = state
        return jnp.logical_and(i < 40, jnp.logical_not(r < 0.004))

    def refine(state):
        i, _ = state
        x_ref[...] += mm(x_ref[...], w_ref[...], ((1,), (0,)), lax.Precision.HIGHEST)
        w_ref[...] = residual()
        return i + 1, norm(w_ref[...])

    lax.while_loop(more, refine, (jnp.int32(0), jnp.where(first < 0.5, first, 1.0)))
    x_ref[...] += mm(x_ref[...], w_ref[...], ((1,), (0,)), lax.Precision.HIGHEST)

    x = x_ref[...]
    xh = x.astype(BF16)
    xl = (x - xh.astype(F32)).astype(BF16)
    innov = yz[:, 1].reshape(members, size)
    step = min(256, members)
    for i in range(members // step):
        rows = anom[i * step:(i + 1) * step]
        w = mm(rows, xh, ((1,), (0,))) + mm(rows, xl, ((1,), (0,)))
        wh = w.astype(BF16)
        wl = (w - wh.astype(F32)).astype(BF16)
        g = mm(wh, innov, ((1,), (1,))) + mm(wl, innov, ((1,), (1,)))
        gain[i * step:(i + 1) * step, :] = g.astype(BF16)


def patch_gain(yz):
    n, _, part, size = yz.shape
    members = n * part
    return pl.pallas_call(
        gain_kernel,
        out_shape=jax.ShapeDtypeStruct((members, members), BF16),
        in_specs=[VMEM_SPEC],
        out_specs=VMEM_SPEC,
        scratch_shapes=[pltpu.VMEM((size, size), F32)] * 3,
        cost_estimate=pl.CostEstimate(flops=40 * 10**9, bytes_accessed=4 * 10**6, transcendentals=0),
    )(yz)


def update_kernel(n, links, own, before, after, prior, out, ready, send_sem, recv_sem, local_sem):
    me = lax.axis_index("mem")
    members, points = prior.shape
    part = members // n
    chunk = max(part, min(128, members))
    inside = chunk // part
    chunks = members // chunk
    barrier = pltpu.get_barrier_semaphore()

    def greet(s, carry):
        pl.semaphore_signal(barrier, inc=1, device_id={"mem": lax.rem(me + s, n)}, device_id_type=MESH)
        return carry

    lax.fori_loop(1, n, greet, 0)
    pl.semaphore_wait(barrier, n - 1)

    up = 0.5 + 0.5 * links[0, 0].astype(F32)
    low = 0.5 + 0.5 * links[0, 1].astype(F32)
    scale = 1.0 + up + low

    def copy(d):
        return pltpu.make_async_remote_copy(
            src_ref=ready.at[d], dst_ref=out.at[me], send_sem=send_sem.at[d], recv_sem=recv_sem.at[me],
            device_id={"mem": d}, device_id_type=MESH)

    keep = pltpu.make_async_copy(ready.at[me], out.at[me], local_sem)

    def piece(s, carry):
        c = lax.rem(me // inside + s + 1, chunks)
        cols = pl.ds(pl.multiple_of(c * chunk, chunk), chunk)
        smooth = own[:, cols].astype(F32) + up * before[:, cols].astype(F32) + low * after[:, cols].astype(F32)
        smooth = (smooth / scale).astype(BF16)
        new = mm(smooth, prior[...], ((0,), (0,)))
        new = (prior[cols, :].astype(F32) + new).astype(BF16)
        for i in range(inside):
            d = c * inside + i
            ready[d] = new[i * part:(i + 1) * part, :]

            @pl.when(d != me)
            def _():
                copy(d).start()
        return carry

    lax.fori_loop(0, chunks, piece, 0)
    keep.start()

    def finish(s, carry):
        d = lax.rem(me + s, n)
        copy(d).wait_send()
        pltpu.make_async_remote_copy(
            src_ref=ready.at[d], dst_ref=out.at[d], send_sem=send_sem.at[d], recv_sem=recv_sem.at[d],
            device_id={"mem": d}, device_id_type=MESH).wait_recv()
        return carry

    lax.fori_loop(1, n, finish, 0)
    keep.wait()


def update(links, own, before, after, prior, n):
    members, points = prior.shape
    part = members // n
    return pl.pallas_call(
        functools.partial(update_kernel, n),
        out_shape=jax.ShapeDtypeStruct((n, part, points), BF16),
        in_specs=[SMEM_SPEC] + [VMEM_SPEC] * 4,
        out_specs=ANY_SPEC,
        scratch_shapes=[
            pltpu.VMEM((n, part, points), BF16),
            pltpu.SemaphoreType.DMA((n,)),
            pltpu.SemaphoreType.DMA((n,)),
            pltpu.SemaphoreType.DMA,
        ],
        compiler_params=pltpu.CompilerParams(collective_id=0, has_side_effects=True),
        cost_estimate=pl.CostEstimate(flops=2 * members * members * points, bytes_accessed=10**7, transcendentals=0),
    )(links, own, before, after, prior)


def shifted(x, axis, by):
    count = lax.axis_size(axis)
    pairs = [(i, i + by) for i in range(count) if 0 <= i + by < count]
    return lax.ppermute(x, axis, pairs)


def forecast(ensemble, diffusivity, zonal_velocity):
    rows = jnp.transpose(ensemble, (1, 0, 2))
    before = shifted(rows[-1:], "slab", 1)
    after = shifted(rows[:1], "slab", -1)
    padded = jnp.concatenate([before, rows, after], axis=0)
    values = rows.astype(F32)
    north, south = padded[:-2].astype(F32), padded[2:].astype(F32)
    east, west = jnp.roll(values, -1, axis=2), jnp.roll(values, 1, axis=2)
    tendency = diffusivity[:, None, :] * (north + south + east + west - 4.0 * values) - zonal_velocity[:, None, :] * (east - west) * 0.5
    return (values + tendency).astype(BF16)


def local(ensemble, diffusivity, zonal_velocity, obs_anomalies, innovations, block_lists, block_counts, patch_links):
    n = lax.axis_size("mem")
    swap = functools.partial(lax.all_to_all, axis_name="mem", split_axis=0, concat_axis=0, tiled=True)
    yz = swap(pick(obs_anomalies, innovations, block_lists, block_counts))
    prior = swap(forecast(ensemble, diffusivity, zonal_velocity))
    prior = prior.reshape(-1, prior.shape[-1])
    gain = patch_gain(yz)
    before = shifted(gain, ("slab", "mem"), 1)
    after = shifted(gain, ("slab", "mem"), -1)
    out = update(patch_links, gain, before, after, prior, n)
    return jnp.transpose(out, (1, 0, 2))


def solution(mesh):
    in_specs = (
        P("mem", "slab", None),
        P("slab", None),
        P("slab", None),
        P("mem", "slab", None),
        P("mem", "slab", None),
        P("slab", None),
        P("slab"),
        P(("slab", "mem"), None),
    )
    return jax.shard_map(local, mesh=mesh, in_specs=in_specs, out_specs=P("mem", "slab", None), check_vma=False)
```

```python
import functools

import jax
import jax.numpy as jnp
from jax import lax
from jax.experimental import pallas as pl
from jax.experimental.pallas import tpu as pltpu
from jax.sharding import PartitionSpec as P

F32, BF16 = jnp.float32, jnp.bfloat16
VMEM_SPEC = pl.BlockSpec(memory_space=pltpu.VMEM)
SMEM_SPEC = pl.BlockSpec(memory_space=pltpu.SMEM)
ANY_SPEC = pl.BlockSpec(memory_space=pl.ANY)
MESH = pl.DeviceIdType.MESH


def mm(a, b, dims, precision=None):
    return lax.dot_general(a, b, (dims, ((), ())), precision=precision, preferred_element_type=F32)


def turned(index, count):
    odd = lax.rem(lax.axis_index("slab"), 2)
    return index + odd * (count - 1 - 2 * index)


def holder(patch, count):
    slab, index = divmod(patch, count)
    return slab * count + (index if slab % 2 == 0 else count - 1 - index)


def pick_kernel(blocks, lists, counts, anom, innov, out, wide):
    width, patches = lists.shape
    members = out.shape[2]
    block = anom.shape[1]
    wide[0] = anom[...].astype(F32)
    wide[1] = innov[...].astype(F32)

    def patch(slot, carry):
        p = turned(slot, patches)
        for j in range(width):
            entry = lists[j, p]
            keep = (j < counts[p]).astype(F32)
            for kind in range(2):
                rows = wide[kind, pl.ds(entry, members, stride=blocks), :]
                out[slot, kind, :, j * block:(j + 1) * block] = (rows * keep).astype(BF16)
        return carry

    lax.fori_loop(0, patches, patch, 0)


def pick(anom, innov, lists, counts):
    members, blocks, block = anom.shape
    patches, width = lists.shape
    return pl.pallas_call(
        functools.partial(pick_kernel, blocks),
        out_shape=jax.ShapeDtypeStruct((patches, 2, members, width * block), BF16),
        in_specs=[SMEM_SPEC, SMEM_SPEC, VMEM_SPEC, VMEM_SPEC],
        out_specs=VMEM_SPEC,
        scratch_shapes=[pltpu.VMEM((2, members * blocks, block), F32)],
    )(lists.T, counts, anom.reshape(-1, block), innov.reshape(-1, block))


def gain_kernel(yz, gain, a_ref, x_ref, w_ref):
    n, _, part, size = yz.shape
    members = n * part
    shift = members - 1.0
    anom = yz[:, 0].reshape(members, size)
    diag = lax.broadcasted_iota(jnp.int32, (size, size), 0) == lax.broadcasted_iota(jnp.int32, (size, size), 1)
    eye = jnp.where(diag, 1.0, 0.0).astype(F32)
    a = mm(anom, anom, ((0,), (0,))) + shift * eye
    a_ref[...] = a
    bound = jnp.max(jnp.sum(jnp.abs(a), axis=0, keepdims=True))
    start = 2.0 / (shift + bound)
    x_ref[...] = (2.0 * start) * eye - (start * start) * a

    def rough(i, carry):
        x = x_ref[...]
        xb = x.astype(BF16)
        r = eye - mm(a_ref[...].astype(BF16), xb, ((1,), (0,)))
        x_ref[...] = x + mm(xb, r.astype(BF16), ((1,), (0,)))
        return carry

    lax.fori_loop(0, 5, rough, 0)

    def norm(r):
        return jnp.max(jnp.sum(jnp.abs(r), axis=0, keepdims=True))

    def residual():
        return eye - mm(a_ref[...], x_ref[...], ((1,), (0,)), lax.Precision.HIGHEST)

    w_ref[...] = residual()
    first = norm(w_ref[...])

    @pl.when(jnp.logical_not(first < 0.5))
    def _():
        x_ref[...] = start * eye
        w_ref[...] = residual()

    def more(state):
        i, r = state
        return jnp.logical_and(i < 40, jnp.logical_not(r < 0.004))

    def refine(state):
        i, _ = state
        x_ref[...] += mm(x_ref[...], w_ref[...], ((1,), (0,)), lax.Precision.HIGHEST)
        w_ref[...] = residual()
        return i + 1, norm(w_ref[...])

    lax.while_loop(more, refine, (jnp.int32(0), jnp.where(first < 0.5, first, 1.0)))
    x_ref[...] += mm(x_ref[...], w_ref[...], ((1,), (0,)), lax.Precision.HIGHEST)

    x = x_ref[...]
    xh = x.astype(BF16)
    xl = (x - xh.astype(F32)).astype(BF16)
    innov = yz[:, 1].reshape(members, size)
    step = min(256, members)
    for i in range(members // step):
        rows = anom[i * step:(i + 1) * step]
        w = mm(rows, xh, ((1,), (0,))) + mm(rows, xl, ((1,), (0,)))
        wh = w.astype(BF16)
        wl = (w - wh.astype(F32)).astype(BF16)
        g = mm(wh, innov, ((1,), (1,))) + mm(wl, innov, ((1,), (1,)))
        gain[i * step:(i + 1) * step, :] = g.astype(BF16)


def patch_gain(yz):
    n, _, part, size = yz.shape
    members = n * part
    return pl.pallas_call(
        gain_kernel,
        out_shape=jax.ShapeDtypeStruct((members, members), BF16),
        in_specs=[VMEM_SPEC],
        out_specs=VMEM_SPEC,
        scratch_shapes=[pltpu.VMEM((size, size), F32)] * 3,
        cost_estimate=pl.CostEstimate(flops=40 * 10**9, bytes_accessed=4 * 10**6, transcendentals=0),
    )(yz)


def update_kernel(n, links, own, before, after, prior, out, ready, send_sem, recv_sem, local_sem):
    me = lax.axis_index("mem")
    members, points = prior.shape
    part = members // n
    chunk = max(part, min(128, members))
    inside = chunk // part
    chunks = members // chunk
    half = chunks // 2
    mine, place = me // inside // half, lax.rem(me // inside, half)
    row = turned(me, n)
    barrier = pltpu.get_barrier_semaphore()

    def greet(s, carry):
        pl.semaphore_signal(barrier, inc=1, device_id={"mem": lax.rem(me + s, n)}, device_id_type=MESH)
        return carry

    lax.fori_loop(1, n, greet, 0)
    pl.semaphore_wait(barrier, n - 1)

    up = 0.5 + 0.5 * links[0, 0].astype(F32)
    low = 0.5 + 0.5 * links[0, 1].astype(F32)
    scale = 1.0 + up + low

    def copy(d):
        return pltpu.make_async_remote_copy(
            src_ref=ready.at[d], dst_ref=out.at[row], send_sem=send_sem.at[d], recv_sem=recv_sem.at[me],
            device_id={"mem": d}, device_id_type=MESH)

    keep = pltpu.make_async_copy(ready.at[me], out.at[row], local_sem)

    def piece(s, carry):
        near = s // half
        side = mine + (1 - near) * (1 - 2 * mine)
        c = side * half + lax.rem(place + s + near, half)
        cols = pl.ds(pl.multiple_of(c * chunk, chunk), chunk)
        smooth = own[:, cols].astype(F32) + up * before[:, cols].astype(F32) + low * after[:, cols].astype(F32)
        smooth = (smooth / scale).astype(BF16)
        new = mm(smooth, prior[...], ((0,), (0,)))
        new = (prior[cols, :].astype(F32) + new).astype(BF16)
        for i in range(inside):
            d = c * inside + i
            ready[d] = new[i * part:(i + 1) * part, :]

            @pl.when(d != me)
            def _():
                copy(d).start()
        return carry

    lax.fori_loop(0, chunks, piece, 0)
    keep.start()

    def finish(s, carry):
        d = lax.rem(me + s, n)
        copy(d).wait_send()
        pltpu.make_async_remote_copy(
            src_ref=ready.at[d], dst_ref=out.at[turned(d, n)], send_sem=send_sem.at[d], recv_sem=recv_sem.at[d],
            device_id={"mem": d}, device_id_type=MESH).wait_recv()
        return carry

    lax.fori_loop(1, n, finish, 0)
    keep.wait()


def update(links, own, before, after, prior, n):
    members, points = prior.shape
    part = members // n
    return pl.pallas_call(
        functools.partial(update_kernel, n),
        out_shape=jax.ShapeDtypeStruct((n, part, points), BF16),
        in_specs=[SMEM_SPEC] + [VMEM_SPEC] * 4,
        out_specs=ANY_SPEC,
        scratch_shapes=[
            pltpu.VMEM((n, part, points), BF16),
            pltpu.SemaphoreType.DMA((n,)),
            pltpu.SemaphoreType.DMA((n,)),
            pltpu.SemaphoreType.DMA,
        ],
        compiler_params=pltpu.CompilerParams(collective_id=0, has_side_effects=True),
        cost_estimate=pl.CostEstimate(flops=2 * members * members * points, bytes_accessed=10**7, transcendentals=0),
    )(links, own, before, after, prior)


def shifted(x, axis, by):
    count = lax.axis_size(axis)
    pairs = [(i, i + by) for i in range(count) if 0 <= i + by < count]
    return lax.ppermute(x, axis, pairs)


def neighbour(x, slabs, count, by):
    total = slabs * count
    pairs = [(holder(p, count), holder(p + by, count)) for p in range(total) if 0 <= p + by < total]
    return lax.ppermute(x, ("slab", "mem"), pairs)


def forecast(ensemble, diffusivity, zonal_velocity):
    rows = jnp.transpose(ensemble, (1, 0, 2))
    before = shifted(rows[-1:], "slab", 1)
    after = shifted(rows[:1], "slab", -1)
    padded = jnp.concatenate([before, rows, after], axis=0)
    odd = lax.rem(lax.axis_index("slab"), 2) == 1
    padded, diffusivity, zonal_velocity = (
        jnp.where(odd, x[::-1], x) for x in (padded, diffusivity, zonal_velocity))
    values = padded[1:-1].astype(F32)
    north, south = padded[:-2].astype(F32), padded[2:].astype(F32)
    east, west = jnp.roll(values, -1, axis=2), jnp.roll(values, 1, axis=2)
    tendency = diffusivity[:, None, :] * (north + south + east + west - 4.0 * values) - zonal_velocity[:, None, :] * (east - west) * 0.5
    return (values + tendency).astype(BF16)


def local(ensemble, diffusivity, zonal_velocity, obs_anomalies, innovations, block_lists, block_counts, patch_links):
    n = lax.axis_size("mem")
    swap = functools.partial(lax.all_to_all, axis_name="mem", split_axis=0, concat_axis=0, tiled=True)
    yz = swap(pick(obs_anomalies, innovations, block_lists, block_counts))
    prior = swap(forecast(ensemble, diffusivity, zonal_velocity))
    prior = prior.reshape(-1, prior.shape[-1])
    gain = patch_gain(yz)
    slabs = lax.axis_size("slab")
    before = neighbour(gain, slabs, n, 1)
    after = neighbour(gain, slabs, n, -1)
    links = lax.ppermute(patch_links, ("slab", "mem"), [(i, holder(i, n)) for i in range(slabs * n)])
    out = update(links, gain, before, after, prior, n)
    return jnp.transpose(out, (1, 0, 2))


def solution(mesh):
    in_specs = (
        P("mem", "slab", None),
        P("slab", None),
        P("slab", None),
        P("mem", "slab", None),
        P("mem", "slab", None),
        P("slab", None),
        P("slab"),
        P(("slab", "mem"), None),
    )
    return jax.shard_map(local, mesh=mesh, in_specs=in_specs, out_specs=P("mem", "slab", None), check_vma=False)
```

```python
import functools

import jax
import jax.numpy as jnp
from jax import lax
from jax.experimental import pallas as pl
from jax.experimental.pallas import tpu as pltpu
from jax.sharding import PartitionSpec as P

F32, BF16 = jnp.float32, jnp.bfloat16
VMEM_SPEC = pl.BlockSpec(memory_space=pltpu.VMEM)
SMEM_SPEC = pl.BlockSpec(memory_space=pltpu.SMEM)
ANY_SPEC = pl.BlockSpec(memory_space=pl.ANY)
MESH = pl.DeviceIdType.MESH


def mm(a, b, dims, precision=None):
    return lax.dot_general(a, b, (dims, ((), ())), precision=precision, preferred_element_type=F32)


def turned(index, count):
    odd = lax.rem(lax.axis_index("slab"), 2)
    return index + odd * (count - 1 - 2 * index)


def holder(patch, count):
    slab, index = divmod(patch, count)
    return slab * count + (index if slab % 2 == 0 else count - 1 - index)


def pick_kernel(blocks, lists, counts, anom, innov, first, second, wide):
    width, patches = lists.shape
    members = first.shape[1]
    block = anom.shape[1]
    wide[0] = anom[...].astype(F32)
    wide[1] = innov[...].astype(F32)

    def patch(slot, carry):
        p = turned(slot, patches)
        for j in range(width):
            entry = lists[j, p]
            keep = (j < counts[p]).astype(F32)
            for kind, out in enumerate((first, second)):
                rows = wide[kind, pl.ds(entry, members, stride=blocks), :]
                out[slot, :, j * block:(j + 1) * block] = (rows * keep).astype(BF16)
        return carry

    lax.fori_loop(0, patches, patch, 0)


def pick(anom, innov, lists, counts):
    members, blocks, block = anom.shape
    patches, width = lists.shape
    return pl.pallas_call(
        functools.partial(pick_kernel, blocks),
        out_shape=[jax.ShapeDtypeStruct((patches, members, width * block), BF16)] * 2,
        in_specs=[SMEM_SPEC, SMEM_SPEC, VMEM_SPEC, VMEM_SPEC],
        out_specs=[VMEM_SPEC] * 2,
        scratch_shapes=[pltpu.VMEM((2, members * blocks, block), F32)],
    )(lists.T, counts, anom.reshape(-1, block), innov.reshape(-1, block))


def weight_kernel(anom, weight, a_ref, x_ref, w_ref):
    members, size = anom.shape
    shift = members - 1.0
    diag = lax.broadcasted_iota(jnp.int32, (size, size), 0) == lax.broadcasted_iota(jnp.int32, (size, size), 1)
    eye = jnp.where(diag, 1.0, 0.0).astype(F32)
    a = mm(anom[...], anom[...], ((0,), (0,))) + shift * eye
    a_ref[...] = a
    bound = jnp.max(jnp.sum(jnp.abs(a), axis=0, keepdims=True))
    start = 2.0 / (shift + bound)
    x_ref[...] = (2.0 * start) * eye - (start * start) * a

    def rough(i, carry):
        x = x_ref[...]
        xb = x.astype(BF16)
        r = eye - mm(a_ref[...].astype(BF16), xb, ((1,), (0,)))
        x_ref[...] = x + mm(xb, r.astype(BF16), ((1,), (0,)))
        return carry

    lax.fori_loop(0, 5, rough, 0)

    def norm(r):
        return jnp.max(jnp.sum(jnp.abs(r), axis=0, keepdims=True))

    def residual():
        return eye - mm(a_ref[...], x_ref[...], ((1,), (0,)), lax.Precision.HIGHEST)

    w_ref[...] = residual()
    first = norm(w_ref[...])

    @pl.when(jnp.logical_not(first < 0.5))
    def _():
        x_ref[...] = start * eye
        w_ref[...] = residual()

    def more(state):
        i, r = state
        return jnp.logical_and(i < 40, jnp.logical_not(r < 0.004))

    def refine(state):
        i, _ = state
        x_ref[...] += mm(x_ref[...], w_ref[...], ((1,), (0,)), lax.Precision.HIGHEST)
        w_ref[...] = residual()
        return i + 1, norm(w_ref[...])

    lax.while_loop(more, refine, (jnp.int32(0), jnp.where(first < 0.5, first, 1.0)))
    x_ref[...] += mm(x_ref[...], w_ref[...], ((1,), (0,)), lax.Precision.HIGHEST)

    x = x_ref[...]
    xh = x.astype(BF16)
    xl = (x - xh.astype(F32)).astype(BF16)
    step = min(256, members)
    for i in range(members // step):
        rows = anom[i * step:(i + 1) * step]
        w = mm(rows, xh, ((1,), (0,))) + mm(rows, xl, ((1,), (0,)))
        wh = w.astype(BF16)
        weight[0, i * step:(i + 1) * step, :] = wh
        weight[1, i * step:(i + 1) * step, :] = (w - wh.astype(F32)).astype(BF16)


def patch_weight(anom):
    members, size = anom.shape
    return pl.pallas_call(
        weight_kernel,
        out_shape=jax.ShapeDtypeStruct((2, members, size), BF16),
        in_specs=[VMEM_SPEC],
        out_specs=VMEM_SPEC,
        scratch_shapes=[pltpu.VMEM((size, size), F32)] * 3,
        cost_estimate=pl.CostEstimate(flops=20 * 10**9, bytes_accessed=4 * 10**6, transcendentals=0),
    )(anom)


def update_kernel(n, slabs, links, weight, innov, states, out, prior, own, before, after, ready,
                  send_f, recv_f, send_g, recv_g, send_d, recv_d, local_sem):
    me, slab = lax.axis_index("mem"), lax.axis_index("slab")
    members, points = prior.shape
    part = members // n
    chunks, _, chunk = own.shape
    inside = chunk // part
    half = chunks // 2
    mine, place = me // inside // half, lax.rem(me // inside, half)
    row = turned(me, n)
    way = 1 - 2 * lax.rem(slab, 2)
    last, first = row // (n - 1), (n - 1 - row) // (n - 1)
    following = {"slab": slab + last, "mem": me + way * (1 - last)}
    previous = {"slab": slab - first, "mem": me - way * (1 - first)}
    total, number = slabs * n, slab * n + row
    has_next, has_prev = number < total - 1, number > 0
    edge_next = last * (1 - slab // (slabs - 1))
    edge_prev = first * (1 - (slabs - 1 - slab) // (slabs - 1))

    barrier = pltpu.get_barrier_semaphore()

    def greet(s, carry):
        pl.semaphore_signal(barrier, inc=1, device_id={"slab": slab, "mem": lax.rem(me + s, n)}, device_id_type=MESH)
        return carry

    lax.fori_loop(1, n, greet, 0)
    for edge, other in ((edge_next, following), (edge_prev, previous)):
        @pl.when(edge == 1)
        def _():
            pl.semaphore_signal(barrier, inc=1, device_id=other, device_id_type=MESH)

    pl.semaphore_wait(barrier, n - 1 + edge_next + edge_prev)

    def span(d):
        return pl.ds(pl.multiple_of(d * part, part), part)

    def remote(src, dst, send, recv, device):
        return pltpu.make_async_remote_copy(
            src_ref=src, dst_ref=dst, send_sem=send, recv_sem=recv, device_id=device, device_id_type=MESH)

    def peer(d):
        return {"slab": slab, "mem": d}

    def far_first(s):
        near = s // half
        side = mine + (1 - near) * (1 - 2 * mine)
        return side * half + lax.rem(place + s + near, half)

    def send_states(s, carry):
        c = far_first(s)
        for i in range(inside):
            d = c * inside + i

            @pl.when(d != me)
            def _():
                remote(states.at[d], prior.at[span(me)], send_f.at[d], recv_f.at[me], peer(d)).start()
        return carry

    lax.fori_loop(0, chunks, send_states, 0)
    prior[span(me), :] = states[me]

    def to_next(c):
        return remote(own.at[c], before.at[c], send_g.at[0, c], recv_g.at[0, c], following)

    def to_prev(c):
        return remote(own.at[c], after.at[c], send_g.at[1, c], recv_g.at[1, c], previous)

    def gains(s, carry):
        c = far_first(s)
        rows = innov[pl.ds(pl.multiple_of(c * chunk, chunk), chunk), :]
        own[c] = (mm(weight[0], rows, ((1,), (1,))) + mm(weight[1], rows, ((1,), (1,)))).astype(BF16)

        @pl.when(has_next)
        def _():
            to_next(c).start()

        @pl.when(has_prev)
        def _():
            to_prev(c).start()
        return carry

    lax.fori_loop(0, chunks, gains, 0)

    @pl.when(jnp.logical_not(has_prev))
    def _():
        before[...] = jnp.zeros_like(before)

    @pl.when(jnp.logical_not(has_next))
    def _():
        after[...] = jnp.zeros_like(after)

    up = 0.5 + 0.5 * links[0, 0].astype(F32)
    low = 0.5 + 0.5 * links[0, 1].astype(F32)
    scale = 1.0 + up + low

    def states_came(s, carry):
        d = lax.rem(me + s, n)
        remote(states.at[d], prior.at[span(d)], send_f.at[d], recv_f.at[d], peer(d)).wait()
        return carry

    lax.fori_loop(1, n, states_came, 0)

    def copy(d):
        return remote(ready.at[d], out.at[row], send_d.at[d], recv_d.at[me], peer(d))

    keep = pltpu.make_async_copy(ready.at[me], out.at[row], local_sem)

    def piece(s, carry):
        c = far_first(s)

        @pl.when(has_next)
        def _():
            to_prev_twin = remote(own.at[c], after.at[c], send_g.at[0, c], recv_g.at[1, c], following)
            to_prev_twin.wait()

        @pl.when(has_prev)
        def _():
            to_next_twin = remote(own.at[c], before.at[c], send_g.at[1, c], recv_g.at[0, c], previous)
            to_next_twin.wait()

        smooth = own[c].astype(F32) + up * before[c].astype(F32) + low * after[c].astype(F32)
        smooth = (smooth / scale).astype(BF16)
        new = mm(smooth, prior[...], ((0,), (0,)))
        rows = prior[pl.ds(pl.multiple_of(c * chunk, chunk), chunk), :]
        new = (rows.astype(F32) + new).astype(BF16)
        for i in range(inside):
            d = c * inside + i
            ready[d] = new[i * part:(i + 1) * part, :]

            @pl.when(d != me)
            def _():
                copy(d).start()
        return carry

    lax.fori_loop(0, chunks, piece, 0)
    keep.start()

    def finish(s, carry):
        d = lax.rem(me + s, n)
        remote(ready.at[d], out.at[turned(d, n)], send_d.at[d], recv_d.at[d], peer(d)).wait()
        return carry

    lax.fori_loop(1, n, finish, 0)
    keep.wait()


def update(links, weight, innov, states, slabs):
    n, part, points = states.shape
    members = n * part
    chunk = max(part, min(128, members))
    gains = pltpu.VMEM((members // chunk, members, chunk), BF16)
    return pl.pallas_call(
        functools.partial(update_kernel, n, slabs),
        out_shape=jax.ShapeDtypeStruct((n, part, points), BF16),
        in_specs=[SMEM_SPEC] + [VMEM_SPEC] * 3,
        out_specs=ANY_SPEC,
        scratch_shapes=[pltpu.VMEM((members, points), BF16), gains, gains, gains, pltpu.VMEM((n, part, points), BF16)]
        + [pltpu.SemaphoreType.DMA((n,))] * 2
        + [pltpu.SemaphoreType.DMA((2, members // chunk))] * 2
        + [pltpu.SemaphoreType.DMA((n,))] * 2
        + [pltpu.SemaphoreType.DMA],
        compiler_params=pltpu.CompilerParams(collective_id=0, has_side_effects=True),
        cost_estimate=pl.CostEstimate(flops=2 * members * members * points, bytes_accessed=10**7, transcendentals=0),
    )(links, weight, innov, states)


def shifted(x, axis, by):
    count = lax.axis_size(axis)
    pairs = [(i, i + by) for i in range(count) if 0 <= i + by < count]
    return lax.ppermute(x, axis, pairs)


def forecast(ensemble, diffusivity, zonal_velocity):
    rows = jnp.transpose(ensemble, (1, 0, 2))
    before = shifted(rows[-1:], "slab", 1)
    after = shifted(rows[:1], "slab", -1)
    padded = jnp.concatenate([before, rows, after], axis=0)
    odd = lax.rem(lax.axis_index("slab"), 2) == 1
    padded, diffusivity, zonal_velocity = (
        jnp.where(odd, x[::-1], x) for x in (padded, diffusivity, zonal_velocity))
    values = padded[1:-1].astype(F32)
    north, south = padded[:-2].astype(F32), padded[2:].astype(F32)
    east, west = jnp.roll(values, -1, axis=2), jnp.roll(values, 1, axis=2)
    tendency = diffusivity[:, None, :] * (north + south + east + west - 4.0 * values) - zonal_velocity[:, None, :] * (east - west) * 0.5
    return (values + tendency).astype(BF16)


def local(ensemble, diffusivity, zonal_velocity, obs_anomalies, innovations, block_lists, block_counts, patch_links):
    n = lax.axis_size("mem")
    swap = functools.partial(lax.all_to_all, axis_name="mem", split_axis=0, concat_axis=0, tiled=True)
    slabs = lax.axis_size("slab")
    links = lax.ppermute(patch_links, ("slab", "mem"), [(i, holder(i, n)) for i in range(slabs * n)])
    anom, innov = pick(obs_anomalies, innovations, block_lists, block_counts)
    states = forecast(ensemble, diffusivity, zonal_velocity)
    anom = swap(anom)
    anom, innov = lax.optimization_barrier((anom, innov))
    innov = swap(innov)
    size = anom.shape[-1]
    weight = patch_weight(anom.reshape(-1, size))
    out = update(links, weight, innov.reshape(-1, size), states, slabs)
    return jnp.transpose(out, (1, 0, 2))


def solution(mesh):
    in_specs = (
        P("mem", "slab", None),
        P("slab", None),
        P("slab", None),
        P("mem", "slab", None),
        P("mem", "slab", None),
        P("slab", None),
        P("slab"),
        P(("slab", "mem"), None),
    )
    return jax.shard_map(local, mesh=mesh, in_specs=in_specs, out_specs=P("mem", "slab", None), check_vma=False)
```

```python
import functools

import jax
import jax.numpy as jnp
from jax import lax
from jax.experimental import pallas as pl
from jax.experimental.pallas import tpu as pltpu
from jax.sharding import PartitionSpec as P

F32, BF16 = jnp.float32, jnp.bfloat16
VMEM_SPEC = pl.BlockSpec(memory_space=pltpu.VMEM)
SMEM_SPEC = pl.BlockSpec(memory_space=pltpu.SMEM)
ANY_SPEC = pl.BlockSpec(memory_space=pl.ANY)
MESH = pl.DeviceIdType.MESH


def mm(a, b, dims, precision=None):
    return lax.dot_general(a, b, (dims, ((), ())), precision=precision, preferred_element_type=F32)


def turned(index, count):
    odd = lax.rem(lax.axis_index("slab"), 2)
    return index + odd * (count - 1 - 2 * index)


def holder(patch, count):
    slab, index = divmod(patch, count)
    return slab * count + (index if slab % 2 == 0 else count - 1 - index)


def pick_kernel(blocks, lists, counts, anom, innov, out, wide):
    width, patches = lists.shape
    members = out.shape[2]
    block = anom.shape[1]
    wide[0] = anom[...].astype(F32)
    wide[1] = innov[...].astype(F32)

    def patch(slot, carry):
        p = turned(slot, patches)
        for j in range(width):
            entry = lists[j, p]
            keep = (j < counts[p]).astype(F32)
            for kind in range(2):
                rows = wide[kind, pl.ds(entry, members, stride=blocks), :]
                out[slot, kind, :, j * block:(j + 1) * block] = (rows * keep).astype(BF16)
        return carry

    lax.fori_loop(0, patches, patch, 0)


def pick(anom, innov, lists, counts):
    members, blocks, block = anom.shape
    patches, width = lists.shape
    return pl.pallas_call(
        functools.partial(pick_kernel, blocks),
        out_shape=jax.ShapeDtypeStruct((patches, 2, members, width * block), BF16),
        in_specs=[SMEM_SPEC, SMEM_SPEC, VMEM_SPEC, VMEM_SPEC],
        out_specs=VMEM_SPEC,
        scratch_shapes=[pltpu.VMEM((2, members * blocks, block), F32)],
    )(lists.T, counts, anom.reshape(-1, block), innov.reshape(-1, block))


def weight_kernel(yz, weight, a_ref, x_ref, w_ref):
    n, _, part, size = yz.shape
    members = n * part
    shift = members - 1.0
    anom = yz[:, 0].reshape(members, size)
    diag = lax.broadcasted_iota(jnp.int32, (size, size), 0) == lax.broadcasted_iota(jnp.int32, (size, size), 1)
    eye = jnp.where(diag, 1.0, 0.0).astype(F32)
    a = mm(anom, anom, ((0,), (0,))) + shift * eye
    a_ref[...] = a
    bound = jnp.max(jnp.sum(jnp.abs(a), axis=0, keepdims=True))
    start = 2.0 / (shift + bound)
    x_ref[...] = (2.0 * start) * eye - (start * start) * a

    def rough(i, carry):
        x = x_ref[...]
        xb = x.astype(BF16)
        r = eye - mm(a_ref[...].astype(BF16), xb, ((1,), (0,)))
        x_ref[...] = x + mm(xb, r.astype(BF16), ((1,), (0,)))
        return carry

    lax.fori_loop(0, 5, rough, 0)

    def norm(r):
        return jnp.max(jnp.sum(jnp.abs(r), axis=0, keepdims=True))

    def residual():
        return eye - mm(a_ref[...], x_ref[...], ((1,), (0,)), lax.Precision.HIGHEST)

    w_ref[...] = residual()
    first = norm(w_ref[...])

    @pl.when(jnp.logical_not(first < 0.5))
    def _():
        x_ref[...] = start * eye
        w_ref[...] = residual()

    def more(state):
        i, r = state
        return jnp.logical_and(i < 40, jnp.logical_not(r < 0.004))

    def refine(state):
        i, _ = state
        x_ref[...] += mm(x_ref[...], w_ref[...], ((1,), (0,)), lax.Precision.HIGHEST)
        w_ref[...] = residual()
        return i + 1, norm(w_ref[...])

    lax.while_loop(more, refine, (jnp.int32(0), jnp.where(first < 0.5, first, 1.0)))
    x_ref[...] += mm(x_ref[...], w_ref[...], ((1,), (0,)), lax.Precision.HIGHEST)

    x = x_ref[...]
    xh = x.astype(BF16)
    xl = (x - xh.astype(F32)).astype(BF16)
    step = min(256, members)
    for i in range(members // step):
        rows = anom[i * step:(i + 1) * step]
        w = mm(rows, xh, ((1,), (0,))) + mm(rows, xl, ((1,), (0,)))
        wh = w.astype(BF16)
        weight[0, i * step:(i + 1) * step, :] = wh
        weight[1, i * step:(i + 1) * step, :] = (w - wh.astype(F32)).astype(BF16)


def patch_weight(yz):
    n, _, part, size = yz.shape
    members = n * part
    return pl.pallas_call(
        weight_kernel,
        out_shape=jax.ShapeDtypeStruct((2, members, size), BF16),
        in_specs=[VMEM_SPEC],
        out_specs=VMEM_SPEC,
        scratch_shapes=[pltpu.VMEM((size, size), F32)] * 3,
        cost_estimate=pl.CostEstimate(flops=40 * 10**9, bytes_accessed=4 * 10**6, transcendentals=0),
    )(yz)


def update_kernel(n, slabs, links, weight, innov, prior, out, own, before, after, ready,
                  send_g, recv_g, send_d, recv_d, local_sem):
    me, slab = lax.axis_index("mem"), lax.axis_index("slab")
    members, points = prior.shape
    part = members // n
    chunks, _, chunk = own.shape
    inside = chunk // part
    half = chunks // 2
    mine, place = me // inside // half, lax.rem(me // inside, half)
    row = turned(me, n)
    way = 1 - 2 * lax.rem(slab, 2)
    last, first = row // (n - 1), (n - 1 - row) // (n - 1)
    following = {"slab": slab + last, "mem": me + way * (1 - last)}
    previous = {"slab": slab - first, "mem": me - way * (1 - first)}
    total, number = slabs * n, slab * n + row
    has_next, has_prev = number < total - 1, number > 0
    edge_next = last * (1 - slab // (slabs - 1))
    edge_prev = first * (1 - (slabs - 1 - slab) // (slabs - 1))

    barrier = pltpu.get_barrier_semaphore()

    def greet(s, carry):
        pl.semaphore_signal(barrier, inc=1, device_id={"slab": slab, "mem": lax.rem(me + s, n)}, device_id_type=MESH)
        return carry

    lax.fori_loop(1, n, greet, 0)
    for edge, other in ((edge_next, following), (edge_prev, previous)):
        @pl.when(edge == 1)
        def _():
            pl.semaphore_signal(barrier, inc=1, device_id=other, device_id_type=MESH)

    pl.semaphore_wait(barrier, n - 1 + edge_next + edge_prev)

    def remote(src, dst, send, recv, device):
        return pltpu.make_async_remote_copy(
            src_ref=src, dst_ref=dst, send_sem=send, recv_sem=recv, device_id=device, device_id_type=MESH)

    def peer(d):
        return {"slab": slab, "mem": d}

    def far_first(s):
        near = s // half
        side = mine + (1 - near) * (1 - 2 * mine)
        return side * half + lax.rem(place + s + near, half)

    def to_next(c):
        return remote(own.at[c], before.at[c], send_g.at[0, c], recv_g.at[0, c], following)

    def to_prev(c):
        return remote(own.at[c], after.at[c], send_g.at[1, c], recv_g.at[1, c], previous)

    def gains(s, carry):
        c = far_first(s)
        rows = innov[pl.ds(c * (chunk // part), chunk // part), 1].reshape(chunk, innov.shape[-1])
        own[c] = (mm(weight[0], rows, ((1,), (1,))) + mm(weight[1], rows, ((1,), (1,)))).astype(BF16)

        @pl.when(has_next)
        def _():
            to_next(c).start()

        @pl.when(has_prev)
        def _():
            to_prev(c).start()
        return carry

    lax.fori_loop(0, chunks, gains, 0)

    @pl.when(jnp.logical_not(has_prev))
    def _():
        before[...] = jnp.zeros_like(before)

    @pl.when(jnp.logical_not(has_next))
    def _():
        after[...] = jnp.zeros_like(after)

    up = 0.5 + 0.5 * links[0, 0].astype(F32)
    low = 0.5 + 0.5 * links[0, 1].astype(F32)
    scale = 1.0 + up + low

    def copy(d):
        return remote(ready.at[d], out.at[row], send_d.at[d], recv_d.at[me], peer(d))

    keep = pltpu.make_async_copy(ready.at[me], out.at[row], local_sem)

    def piece(s, carry):
        c = far_first(s)

        @pl.when(has_next)
        def _():
            to_prev_twin = remote(own.at[c], after.at[c], send_g.at[0, c], recv_g.at[1, c], following)
            to_prev_twin.wait()

        @pl.when(has_prev)
        def _():
            to_next_twin = remote(own.at[c], before.at[c], send_g.at[1, c], recv_g.at[0, c], previous)
            to_next_twin.wait()

        smooth = own[c].astype(F32) + up * before[c].astype(F32) + low * after[c].astype(F32)
        smooth = (smooth / scale).astype(BF16)
        new = mm(smooth, prior[...], ((0,), (0,)))
        rows = prior[pl.ds(pl.multiple_of(c * chunk, chunk), chunk), :]
        new = (rows.astype(F32) + new).astype(BF16)
        for i in range(inside):
            d = c * inside + i
            ready[d] = new[i * part:(i + 1) * part, :]

            @pl.when(d != me)
            def _():
                copy(d).start()
        return carry

    lax.fori_loop(0, chunks, piece, 0)
    keep.start()

    def finish(s, carry):
        d = lax.rem(me + s, n)
        remote(ready.at[d], out.at[turned(d, n)], send_d.at[d], recv_d.at[d], peer(d)).wait()
        return carry

    lax.fori_loop(1, n, finish, 0)
    keep.wait()


def update(links, weight, innov, prior, n, slabs):
    members, points = prior.shape
    part = members // n
    chunk = max(part, min(128, members))
    gains = pltpu.VMEM((members // chunk, members, chunk), BF16)
    return pl.pallas_call(
        functools.partial(update_kernel, n, slabs),
        out_shape=jax.ShapeDtypeStruct((n, part, points), BF16),
        in_specs=[SMEM_SPEC] + [VMEM_SPEC] * 3,
        out_specs=ANY_SPEC,
        scratch_shapes=[gains, gains, gains, pltpu.VMEM((n, part, points), BF16)]
        + [pltpu.SemaphoreType.DMA((2, members // chunk))] * 2
        + [pltpu.SemaphoreType.DMA((n,))] * 2
        + [pltpu.SemaphoreType.DMA],
        compiler_params=pltpu.CompilerParams(collective_id=0, has_side_effects=True),
        cost_estimate=pl.CostEstimate(flops=2 * members * members * points, bytes_accessed=10**7, transcendentals=0),
    )(links, weight, innov, prior)


def shifted(x, axis, by):
    count = lax.axis_size(axis)
    pairs = [(i, i + by) for i in range(count) if 0 <= i + by < count]
    return lax.ppermute(x, axis, pairs)


def forecast(ensemble, diffusivity, zonal_velocity):
    rows = jnp.transpose(ensemble, (1, 0, 2))
    before = shifted(rows[-1:], "slab", 1)
    after = shifted(rows[:1], "slab", -1)
    padded = jnp.concatenate([before, rows, after], axis=0)
    odd = lax.rem(lax.axis_index("slab"), 2) == 1
    padded, diffusivity, zonal_velocity = (
        jnp.where(odd, x[::-1], x) for x in (padded, diffusivity, zonal_velocity))
    values = padded[1:-1].astype(F32)
    north, south = padded[:-2].astype(F32), padded[2:].astype(F32)
    east, west = jnp.roll(values, -1, axis=2), jnp.roll(values, 1, axis=2)
    tendency = diffusivity[:, None, :] * (north + south + east + west - 4.0 * values) - zonal_velocity[:, None, :] * (east - west) * 0.5
    return (values + tendency).astype(BF16)


def local(ensemble, diffusivity, zonal_velocity, obs_anomalies, innovations, block_lists, block_counts, patch_links):
    n = lax.axis_size("mem")
    swap = functools.partial(lax.all_to_all, axis_name="mem", split_axis=0, concat_axis=0, tiled=True)
    slabs = lax.axis_size("slab")
    links = lax.ppermute(patch_links, ("slab", "mem"), [(i, holder(i, n)) for i in range(slabs * n)])
    yz = swap(pick(obs_anomalies, innovations, block_lists, block_counts))
    prior = swap(forecast(ensemble, diffusivity, zonal_velocity))
    weight = patch_weight(yz)
    out = update(links, weight, yz, prior.reshape(-1, prior.shape[-1]), n, slabs)
    return jnp.transpose(out, (1, 0, 2))


def solution(mesh):
    in_specs = (
        P("mem", "slab", None),
        P("slab", None),
        P("slab", None),
        P("mem", "slab", None),
        P("mem", "slab", None),
        P("slab", None),
        P("slab"),
        P(("slab", "mem"), None),
    )
    return jax.shard_map(local, mesh=mesh, in_specs=in_specs, out_specs=P("mem", "slab", None), check_vma=False)
```
